256 devices in a mesh: dp: 4 (over z_lo, core), seq: 64 (over y, x, z_hi).
Axes of the slice: x: 4, y: 4, z: 8 (z_hi: 4, z_lo: 2; z = z_hi * 2 + z_lo), core: 2. Of those that a mesh axis runs over, the one named last changes fastest.
Arguments:
- traces_in: bfloat16 [8, 512, 512, 128], P('dp', 'seq'), may hold values from -6 to 6
- w_value: bfloat16 [128, 128], replicated, may hold values from -0.5 to 0.5
- w_gate: bfloat16 [128, 128], replicated, may hold values from -0.5 to 0.5
- first_blocks: bfloat16 [512, 512, 512], P('seq', 'dp'), may hold values from -0.25 to 0.25
- second_blocks: bfloat16 [512, 512, 512], P('seq', 'dp'), may hold values from -0.25 to 0.25
- cotangent: bfloat16 [8, 512, 512, 128], P('dp', 'seq'), may hold values from -6 to 6
Outputs:
- mixed: bfloat16 [8, 512, 512, 128], P('dp', 'seq')
- grad_in: bfloat16 [8, 512, 512, 128], P('dp', 'seq')
- grad_first: bfloat16 [512, 512, 512], P('seq', 'dp')
- grad_second: bfloat16 [512, 512, 512], P('seq', 'dp')
The draws below stay inside these ranges and needn't reach their ends.
All inputs are finite; a program needn't handle non-finite values.
Results may differ from the reference program's by a relative error of at most 0.015.
Values may be sent and summed in bfloat16 or wider, within the bound.
A program may use at most 128 MiB of HBM per device.

```python
import jax
import jax.numpy as jnp
from jax import lax

P_SIZE = 512
Q = 512
C = 128
TRACES = 8


def steps_of(key, extent, pieces, smallest, high):
    def one(position, parts):
        heights = jax.random.uniform(jax.random.fold_in(jax.random.fold_in(key, 6), position), (parts,), jnp.float32, smallest / len(pieces), high / len(pieces))
        return jnp.repeat(jnp.exp(heights), extent[position] // parts).reshape((-1,) + (1,) * (len(extent) - position - 1))

    gain = one(*pieces[0])
    for cut in pieces[1:]:
        gain = gain * one(*cut)
    return gain


def gaussian(own_key, dims, scale, most, pieces=(), dtype=jnp.bfloat16):
    result = scale * jax.random.normal(own_key, dims, jnp.float32)
    if pieces:
        result = result * steps_of(own_key, dims, pieces, -0.22, 0.18)
    return jnp.clip(result, -most, most).astype(dtype)


def setup_inputs(seed: int = 0) -> dict:
    streams_of = jax.random.split(jax.random.key(seed), 7)
    return {
        "traces_in": gaussian(streams_of[0], (TRACES, P_SIZE, Q, C), 1.0, 6.0, ((0, 4), (1, 64))),
        "w_value": gaussian(streams_of[1], (C, C), C ** -0.5, 0.5),
        "w_gate": gaussian(streams_of[2], (C, C), C ** -0.5, 0.5),
        "first_blocks": gaussian(streams_of[3], (P_SIZE, Q, Q), Q ** -0.5, 0.25, ((0, 64), (1, 4))),
        "second_blocks": gaussian(streams_of[4], (Q, P_SIZE, P_SIZE), P_SIZE ** -0.5, 0.25, ((0, 64), (1, 4))),
        "cotangent": gaussian(streams_of[5], (TRACES, P_SIZE, Q, C), 1.0, 6.0, ((0, 4), (1, 64))),
    }


def reference(traces_in, w_value, w_gate, first_blocks, second_blocks, cotangent):
    first_f = first_blocks.astype(jnp.float32)
    second_f = second_blocks.astype(jnp.float32)

    def one_trace(carry, inputs):
        acc_first, acc_second = carry
        trace, grad_out = inputs
        flat = trace.reshape(P_SIZE * Q, C)
        values = jnp.dot(flat, w_value, preferred_element_type=jnp.float32).astype(jnp.bfloat16).reshape(P_SIZE, Q, C)
        gates = jnp.dot(flat, w_gate, preferred_element_type=jnp.float32).reshape(P_SIZE, Q, C)
        sig = jax.nn.sigmoid(gates)
        act = gates * sig
        rowmix = jnp.einsum('pij,pjc->pic', first_f, values.astype(jnp.float32)).astype(jnp.bfloat16)
        colmix = jnp.einsum('qij,jqc->iqc', second_f, rowmix.astype(jnp.float32)).astype(jnp.bfloat16)
        colf = colmix.astype(jnp.float32)
        mixed = (colf * act).astype(jnp.bfloat16)
        gradf = grad_out.astype(jnp.float32)
        d_col = (gradf * act).astype(jnp.bfloat16)
        d_gate = (gradf * colf * sig * (1.0 + gates * (1.0 - sig))).astype(jnp.bfloat16)
        d_row = jnp.einsum('qij,iqc->jqc', second_f, d_col.astype(jnp.float32)).astype(jnp.bfloat16)
        acc_second = acc_second + jnp.einsum('iqc,jqc->qij', d_col.astype(jnp.float32), rowmix.astype(jnp.float32))
        d_val = jnp.einsum('pij,pic->pjc', first_f, d_row.astype(jnp.float32)).astype(jnp.bfloat16)
        acc_first = acc_first + jnp.einsum('pic,pjc->pij', d_row.astype(jnp.float32), values.astype(jnp.float32))
        grad_in = jnp.dot(d_val.reshape(P_SIZE * Q, C), w_value.T, preferred_element_type=jnp.float32)
        grad_in = grad_in + jnp.dot(d_gate.reshape(P_SIZE * Q, C), w_gate.T, preferred_element_type=jnp.float32)
        return (acc_first, acc_second), (mixed, grad_in.astype(jnp.bfloat16).reshape(P_SIZE, Q, C))

    start = (jnp.zeros((P_SIZE, Q, Q), jnp.float32), jnp.zeros((Q, P_SIZE, P_SIZE), jnp.float32))
    (acc_first, acc_second), (mixed, grad_in) = lax.scan(one_trace, start, (traces_in, cotangent))
    grad_first = (acc_first / TRACES).astype(jnp.bfloat16)
    grad_second = (acc_second / TRACES).astype(jnp.bfloat16)
    return (mixed, grad_in, grad_first, grad_second)
```

```python
import jax
import jax.numpy as jnp
from jax import lax
from jax.experimental import pallas as pl
from jax.experimental.pallas import tpu as pltpu
from jax.sharding import PartitionSpec as P

MESH = pl.DeviceIdType.MESH
BF = jnp.bfloat16
F32 = jnp.float32


def exchange_kernel(x_ref, o_ref, send_sem, recv_sem, own_sem):
    n = x_ref.shape[0]
    width = lax.axis_size("dp")
    me = lax.axis_index("seq") * width + lax.axis_index("dp")

    def device(k):
        d = lax.rem(me + k, n)
        return d, (lax.rem(d, width), d // width)

    barrier = pltpu.get_barrier_semaphore()

    def greet(k, carry):
        pl.semaphore_signal(barrier, inc=1, device_id=device(k)[1], device_id_type=MESH)
        return carry

    lax.fori_loop(1, n, greet, 0)
    own = pltpu.make_async_copy(x_ref.at[me], o_ref.at[me], own_sem)
    own.start()
    pl.semaphore_wait(barrier, n - 1)

    def send(k, carry):
        d, where = device(k)
        pltpu.make_async_remote_copy(
            x_ref.at[d], o_ref.at[me], send_sem, recv_sem, device_id=where, device_id_type=MESH
        ).start()
        return carry

    lax.fori_loop(1, n, send, 0)
    own.wait()
    rest = pl.ds(0, n - 1)
    pltpu.make_async_copy(x_ref.at[rest], o_ref.at[rest], recv_sem).wait()
    pltpu.make_async_copy(x_ref.at[rest], o_ref.at[rest], send_sem).wait()


def exchange(x):
    return pl.pallas_call(
        exchange_kernel,
        out_shape=jax.ShapeDtypeStruct(x.shape, x.dtype),
        in_specs=[pl.BlockSpec(memory_space=pltpu.VMEM)],
        out_specs=pl.BlockSpec(memory_space=pltpu.VMEM),
        scratch_shapes=[pltpu.SemaphoreType.DMA] * 3,
        cost_estimate=pl.CostEstimate(flops=0, bytes_accessed=150_000_000, transcendentals=0),
        compiler_params=pltpu.CompilerParams(
            collective_id=1, has_side_effects=True, vmem_limit_bytes=16 << 20
        ),
    )(x)


def on_device(traces_in, w_value, w_gate, first_blocks, second_blocks, cotangent):
    dp, seq = lax.axis_size("dp"), lax.axis_size("seq")
    n = dp * seq
    traces, rows, columns, channels = traces_in.shape
    mine = columns // n

    def to_columns(x):
        x = x.reshape(traces, rows, n, mine, channels).transpose(2, 0, 3, 1, 4)
        x = exchange(x.reshape(n, traces * mine, rows, channels))
        return x.reshape(seq, dp, traces, mine, rows, channels)

    def to_rows(x):
        x = exchange(x.reshape(n, traces * mine, rows, channels))
        x = x.reshape(n, traces, mine, rows, channels).transpose(1, 3, 0, 2, 4)
        return x.reshape(traces, rows, columns, channels)

    gates = jnp.einsum("tpqc,cd->tpqd", traces_in, w_gate, preferred_element_type=F32)
    sig = jax.nn.sigmoid(gates)
    act = gates * sig
    gradf = cotangent.astype(F32)
    d_col = (gradf * act).astype(BF)
    full_first = lax.all_gather(first_blocks, "dp", axis=1, tiled=True)
    cotan_cols = to_columns(d_col)
    values = jnp.einsum("tpqc,cd->tpqd", traces_in, w_value, preferred_element_type=F32).astype(BF)
    rowmix = jnp.einsum("pij,tpjc->tpic", full_first, values, preferred_element_type=F32).astype(BF)
    rowmix, cotan_cols = lax.optimization_barrier((rowmix, cotan_cols))
    second = lax.all_to_all(second_blocks, "dp", split_axis=0, concat_axis=1, tiled=True)
    cols = to_columns(rowmix)
    split = second.reshape(mine, seq, rows, columns)
    split_j = second.reshape(mine, columns, seq, rows)
    d_row_cols = jnp.einsum("qspj,sdtqpc->qjdtc", split, cotan_cols, preferred_element_type=F32).astype(BF)

    def chunks(x):
        x = x.reshape(mine, seq, rows, dp, traces, channels)
        return x.transpose(1, 3, 4, 0, 2, 5)

    d_row_chunks, cols = lax.optimization_barrier((chunks(d_row_cols), cols))
    d_row = to_rows(d_row_chunks)
    colmix_cols = jnp.einsum("qisp,sdtqpc->qidtc", split_j, cols, preferred_element_type=F32).astype(BF)
    colmix_chunks, d_row = lax.optimization_barrier((chunks(colmix_cols), d_row))
    first_part = jnp.einsum("tpic,tpjc->pij", d_row, values, preferred_element_type=F32)
    first_sum = lax.psum_scatter(first_part.astype(BF), "dp", scatter_dimension=1, tiled=True)
    trace_count = traces * dp
    grad_first = (first_sum.astype(F32) / trace_count).astype(BF)
    colmix = to_rows(colmix_chunks)
    grad_second = jnp.einsum(
        "sdtqpc,SdtqPc->qspSP", cotan_cols, cols, preferred_element_type=F32
    ).reshape(mine, columns, columns)
    grad_second = (grad_second / trace_count).astype(BF)
    grad_second = lax.all_to_all(grad_second, "dp", split_axis=1, concat_axis=0, tiled=True)
    colf = colmix.astype(F32)
    mixed = (colf * act).astype(BF)
    d_gate = (gradf * colf * sig * (1.0 + gates * (1.0 - sig))).astype(BF)
    d_val = jnp.einsum("pij,tpic->tpjc", full_first, d_row, preferred_element_type=F32).astype(BF)
    grad_in = jnp.einsum("tpqd,cd->tpqc", d_val, w_value, preferred_element_type=F32)
    grad_in = (
        grad_in + jnp.einsum("tpqd,cd->tpqc", d_gate, w_gate, preferred_element_type=F32)
    ).astype(BF)
    return (mixed, grad_in, grad_first, grad_second)


def solution(mesh):
    big, weight = P("dp", "seq", None, None), P("seq", "dp", None)
    return jax.shard_map(
        on_device,
        mesh=mesh,
        in_specs=(big, P(), P(), weight, weight, big),
        out_specs=(big, big, weight, weight),
        check_vma=False,
    )
```

```python
import jax
import jax.numpy as jnp
from jax import lax
from jax.experimental import pallas as pl
from jax.experimental.pallas import tpu as pltpu
from jax.sharding import PartitionSpec as P

MESH = pl.DeviceIdType.MESH
BF = jnp.bfloat16
F32 = jnp.float32
NT = (((1,), (1,)), ((), ()))
TN = (((0,), (0,)), ((), ()))
NN = (((1,), (0,)), ((), ()))


def dot(a, b, dims=NN):
    return lax.dot_general(a, b, dims, preferred_element_type=F32)


def kernel(
    x_hbm, wv_hbm, wg_hbm, first_hbm, second_hbm, cot_hbm,
    mixed_hbm, gin_hbm, gf_hbm, gs_hbm,
    x, wv, wg, cot, val, act, slope, part, first, second, tmp,
    send_a, send_b, cols_a, cols_b, send_c, send_d, rows_c, rows_d,
    gf_tmp, gf_own, gf_near, gf_near_in, gf_far, gf_far_in, gs,
    in_sem, f_send, f_recv, s_send, s_recv, ex_send, ex_recv, ex_own,
    near_send, near_recv, far_send, far_recv, gs_send, gs_recv, gs_own, out_sem,
):
    width, length = lax.axis_size("dp"), lax.axis_size("seq")
    n = width * length
    traces, rows, columns, channels = x.shape
    mine = columns // n
    share = columns // width
    d, s = lax.axis_index("dp"), lax.axis_index("seq")
    me = s * width + d
    near = d + 1 - 2 * lax.rem(d, 2)
    far = lax.rem(d + 2, width)
    cross = lax.rem(near + 2, width)

    loads = [
        pltpu.make_async_copy(a, b, in_sem.at[i])
        for i, (a, b) in enumerate(
            [
                (x_hbm, x), (cot_hbm, cot), (wg_hbm, wg), (wv_hbm, wv),
                (first_hbm, first.at[:, pl.ds(pl.multiple_of(share * d, share), share), :]),
                (
                    second_hbm.at[pl.ds(mine * d, mine)],
                    second.at[:, pl.ds(pl.multiple_of(share * d, share), share), :],
                ),
            ]
        )
    ]
    for load in loads:
        load.start()

    barrier = pltpu.get_barrier_semaphore()

    def greet(k, carry):
        e = lax.rem(me + k, n)
        pl.semaphore_signal(
            barrier, inc=1, device_id=(lax.rem(e, width), e // width), device_id_type=MESH
        )
        return carry

    lax.fori_loop(1, n, greet, 0)
    pl.semaphore_wait(barrier, n - 1)

    def remote(a, b, send, recv, to_dp, to_seq):
        return pltpu.make_async_remote_copy(
            a, b, send, recv, device_id=(to_dp, to_seq), device_id_type=MESH
        )

    def block(owner):
        return pl.ds(pl.multiple_of(share * owner, share), share)

    first_far = remote(first_hbm, first.at[:, block(d), :], f_send.at[0], f_recv.at[0], far, s)
    first_near = remote(first_hbm, first.at[:, block(d), :], f_send.at[1], f_recv.at[1], near, s)
    first_pass = remote(
        first.at[:, block(far), :], first.at[:, block(far), :], f_send.at[2], f_recv.at[2], near, s
    )
    first_far.start()
    first_near.start()

    def pieces_wait(sem):
        rest = send_a.at[:, pl.ds(0, columns - mine)]
        pltpu.make_async_copy(rest, rest, sem).wait()

    def to_columns(buf, out, which):
        def target(o):
            return o.at[pl.ds(traces * d, traces), :, pl.ds(pl.multiple_of(rows * s, rows), rows), :]

        own = pltpu.make_async_copy(
            buf.at[:, pl.ds(mine * me, mine)], target(out), ex_own.at[which]
        )
        own.start()

        def send(k, carry):
            e = lax.rem(me + k, n)
            remote(
                buf.at[:, pl.ds(mine * e, mine)], target(out),
                ex_send.at[which], ex_recv.at[which], lax.rem(e, width), e // width,
            ).start()
            return carry

        lax.fori_loop(1, n, send, 0)
        return own

    def source(buf, e_dp, e_seq):
        return buf.at[
            pl.ds(traces * e_dp, traces), :, pl.ds(pl.multiple_of(rows * e_seq, rows), rows), :
        ]

    def to_rows(buf, out, which, e_dp, first_k):
        def send(k, carry):
            e_seq = lax.rem(s + k, length)
            remote(
                source(buf, e_dp, e_seq), out.at[:, pl.ds(mine * me, mine)],
                ex_send.at[which], ex_recv.at[which], e_dp, e_seq,
            ).start()
            return carry

        lax.fori_loop(first_k, length, send, 0)

    step = 64

    def pack(buf):
        def body(i, carry):
            t, k = i // (columns // step), lax.rem(i, columns // step)
            rows_here = pl.ds(pl.multiple_of(k * step * rows, step * rows), step * rows)
            y = tmp[t, rows_here, :].reshape(step, rows, channels)
            buf[t, pl.ds(k * step, step)] = y.astype(BF)
            return carry

        lax.fori_loop(0, traces * (columns // step), body, 0)

    def unpack(buf):
        def body(i, carry):
            t, k = i // (columns // step), lax.rem(i, columns // step)
            rows_here = pl.ds(pl.multiple_of(k * step * rows, step * rows), step * rows)
            y = buf[t, pl.ds(k * step, step)].astype(F32)
            tmp[t, rows_here, :] = y.reshape(step * rows, channels)
            return carry

        lax.fori_loop(0, traces * (columns // step), body, 0)

    def row(p):
        return pl.ds(p, columns, stride=rows)

    loads[0].wait()
    loads[1].wait()
    loads[2].wait()

    def gate(i, carry):
        t, p = i // rows, lax.rem(i, rows)
        g = dot(x[t, p], wg[...])
        sig = jax.nn.sigmoid(g)
        a = g * sig
        c = cot[t, p].astype(F32)
        act[t, p] = a
        slope[t, p] = c * sig * (1.0 + g * (1.0 - sig))
        tmp[t, row(p), :] = c * a
        return carry

    lax.fori_loop(0, traces * rows, gate, 0)
    pack(send_a)
    own_a = to_columns(send_a, cols_a, 0)

    def second_to(other):
        return remote(
            second_hbm.at[pl.ds(mine * other, mine)], second.at[:, block(d), :],
            s_send, s_recv, other, s,
        )

    for other in (far, cross, near):
        second_to(other).start()

    loads[3].wait()

    def value(i, carry):
        t, p = i // rows, lax.rem(i, rows)
        val[t, p] = dot(x[t, p], wv[...]).astype(BF)
        return carry

    lax.fori_loop(0, traces * rows, value, 0)

    loads[4].wait()
    first_far.wait_recv()
    first_pass.start()
    first_near.wait_recv()
    first_pass.wait_recv()

    def both(ref, p):
        return jnp.concatenate([ref[t, p] for t in range(traces)], axis=1)

    def mix_rows(p, carry):
        o = dot(first[p], both(val, p))
        for t in range(traces):
            tmp[t, row(p), :] = o[:, t * channels : (t + 1) * channels]
        return carry

    lax.fori_loop(0, rows, mix_rows, 0)
    pack(send_b)
    own_b = to_columns(send_b, cols_b, 1)

    loads[5].wait()
    half = second.at[:, pl.ds(0, share * (width - 1)), :]
    pltpu.make_async_copy(half, half, s_recv).wait()

    def columns_back(cols, buf, out, which, dims):
        owns = []
        for k in range(width):
            e_dp = lax.rem(d + k, width)

            def mix(q, carry):
                r = jnp.concatenate(
                    [cols[traces * e_dp + t, q] for t in range(traces)], axis=1
                )
                o = dot(second[q], r, dims).astype(BF)
                for t in range(traces):
                    buf[traces * e_dp + t, q] = o[:, t * channels : (t + 1) * channels]
                return carry

            lax.fori_loop(0, mine, mix, 0)
            if k == 0:
                own = pltpu.make_async_copy(
                    source(buf, d, s), out.at[:, pl.ds(mine * me, mine)], ex_own.at[which]
                )
                own.start()
                owns.append(own)
            to_rows(buf, out, which, e_dp, 1 if k == 0 else 0)
        return owns[0]

    own_a.wait()
    pieces_wait(ex_recv.at[0])
    own_c = columns_back(cols_a, send_c, rows_c, 2, TN)
    own_b.wait()
    pieces_wait(ex_recv.at[1])
    own_d = columns_back(cols_b, send_d, rows_d, 3, NN)

    scale = 1.0 / (traces * width)

    def second_grad(q, carry):
        a = jnp.concatenate([cols_a[t, q] for t in range(traces * width)], axis=1)
        b = jnp.concatenate([cols_b[t, q] for t in range(traces * width)], axis=1)
        gs[q] = (dot(a, b, NT) * scale).astype(BF)
        return carry

    lax.fori_loop(0, mine, second_grad, 0)

    def gs_to(other):
        return remote(
            gs.at[:, block(other), :], gs_hbm.at[pl.ds(mine * d, mine)], gs_send, gs_recv, other, s
        )

    gs_mine = pltpu.make_async_copy(gs.at[:, block(d), :], gs_hbm.at[pl.ds(mine * d, mine)], gs_own)
    gs_mine.start()
    for other in (far, cross, near):
        gs_to(other).start()

    own_c.wait()
    pieces_wait(ex_recv.at[2])
    unpack(rows_c)

    def near_copy(p):
        return remote(gf_near.at[p], gf_near_in.at[p], near_send.at[p], near_recv.at[p], near, s)

    def far_copy(p):
        return remote(gf_far.at[p], gf_far_in.at[p], far_send.at[p], far_recv.at[p], far, s)

    def rows_back(p, carry):
        r = jnp.concatenate([tmp[t, row(p), :] for t in range(traces)], axis=1).astype(BF)
        gf_tmp[...] = dot(r, both(val, p), NT)
        gf_own[p, 0] = gf_tmp[block(d), :]
        gf_own[p, 1] = gf_tmp[block(far), :]
        gf_near[p, 0] = gf_tmp[block(near), :].astype(BF)
        gf_near[p, 1] = gf_tmp[block(cross), :].astype(BF)
        near_copy(p).start()
        v = dot(first[p], r, TN).astype(BF)
        for t in range(traces):
            part[t, p] = dot(v[:, t * channels : (t + 1) * channels], wv[...], NT)
        return carry

    lax.fori_loop(0, rows, rows_back, 0)

    def reduce_near(p, carry):
        near_copy(p).wait_recv()
        gf_far[p] = (gf_own[p, 1] + gf_near_in[p, 1].astype(F32)).astype(BF)
        far_copy(p).start()
        return carry

    lax.fori_loop(0, rows, reduce_near, 0)

    def reduce_far(p, carry):
        far_copy(p).wait_recv()
        near_copy(p).wait_send()
        total = gf_own[p, 0] + gf_near_in[p, 0].astype(F32) + gf_far_in[p].astype(F32)
        gf_near[p, 0] = (total * scale).astype(BF)
        pltpu.make_async_copy(gf_near.at[p, 0], gf_hbm.at[p], out_sem.at[0]).start()
        return carry

    lax.fori_loop(0, rows, reduce_far, 0)

    own_d.wait()
    pieces_wait(ex_recv.at[3])
    unpack(rows_d)

    def finish(i, carry):
        t, p = i // rows, lax.rem(i, rows)
        c = tmp[t, row(p), :]
        x[t, p] = (c * act[t, p]).astype(BF)
        g = (c * slope[t, p]).astype(BF)
        cot[t, p] = (part[t, p] + dot(g, wg[...], NT)).astype(BF)
        pltpu.make_async_copy(x.at[t, p], mixed_hbm.at[t, p], out_sem.at[1]).start()
        pltpu.make_async_copy(cot.at[t, p], gin_hbm.at[t, p], out_sem.at[2]).start()
        return carry

    lax.fori_loop(0, traces * rows, finish, 0)

    first_far.wait_send()
    first_near.wait_send()
    first_pass.wait_send()
    pltpu.make_async_copy(half, half, s_send).wait()
    for which in range(4):
        pieces_wait(ex_send.at[which])

    def sent(p, carry):
        far_copy(p).wait_send()
        return carry

    lax.fori_loop(0, rows, sent, 0)
    gs_mine.wait()
    three = gs.at[:, pl.ds(0, share * (width - 1)), :]
    pltpu.make_async_copy(three, three, gs_send).wait()
    pltpu.make_async_copy(three, three, gs_recv).wait()
    pltpu.make_async_copy(gf_far, gf_hbm, out_sem.at[0]).wait()
    pltpu.make_async_copy(x, mixed_hbm, out_sem.at[1]).wait()
    pltpu.make_async_copy(cot, gin_hbm, out_sem.at[2]).wait()


def on_device(traces_in, w_value, w_gate, first_blocks, second_blocks, cotangent):
    width, length = lax.axis_size("dp"), lax.axis_size("seq")
    traces, rows, columns, channels = traces_in.shape
    mine, share = columns // (width * length), columns // width
    by_row = (traces, columns, rows, channels)
    by_column = (traces * width, mine, rows * length, channels)
    hbm = pl.BlockSpec(memory_space=pl.ANY)
    dma = pltpu.SemaphoreType.DMA
    V = pltpu.VMEM
    shape = traces_in.shape
    return pl.pallas_call(
        kernel,
        out_shape=[
            jax.ShapeDtypeStruct(shape, BF),
            jax.ShapeDtypeStruct(shape, BF),
            jax.ShapeDtypeStruct(first_blocks.shape, BF),
            jax.ShapeDtypeStruct(second_blocks.shape, BF),
        ],
        in_specs=[hbm] * 6,
        out_specs=[hbm] * 4,
        scratch_shapes=[
            V(shape, BF), V(w_value.shape, BF), V(w_gate.shape, BF), V(shape, BF), V(shape, BF),
            V(shape, F32), V(shape, F32), V(shape, F32),
            V((rows, columns, columns), BF), V((mine, columns, columns), BF),
            V((traces, columns * rows, channels), F32),
            V(by_row, BF), V(by_row, BF), V(by_column, BF), V(by_column, BF),
            V(by_column, BF), V(by_column, BF), V(by_row, BF), V(by_row, BF),
            V((columns, columns), F32), V((rows, 2, share, columns), F32),
            V((rows, 2, share, columns), BF), V((rows, 2, share, columns), BF),
            V((rows, share, columns), BF), V((rows, share, columns), BF),
            V((mine, columns, columns), BF),
            dma((6,)), dma((3,)), dma((3,)), dma, dma, dma((4,)), dma((4,)), dma((4,)),
            dma((rows,)), dma((rows,)), dma((rows,)), dma((rows,)), dma, dma, dma, dma((3,)),
        ],
        compiler_params=pltpu.CompilerParams(
            collective_id=1, has_side_effects=True, vmem_limit_bytes=60 << 20
        ),
    )(traces_in, w_value, w_gate, first_blocks, second_blocks, cotangent)


def solution(mesh):
    big, weight = P("dp", "seq", None, None), P("seq", "dp", None)
    return jax.shard_map(
        on_device,
        mesh=mesh,
        in_specs=(big, P(), P(), weight, weight, big),
        out_specs=(big, big, weight, weight),
        check_vma=False,
    )
```

```python
import jax
import jax.numpy as jnp
from jax import lax
from jax.experimental import pallas as pl
from jax.experimental.pallas import tpu as pltpu
from jax.sharding import PartitionSpec as P

MESH = pl.DeviceIdType.MESH
BF = jnp.bfloat16
F32 = jnp.float32
NT = (((1,), (1,)), ((), ()))
TN = (((0,), (0,)), ((), ()))
NN = (((1,), (0,)), ((), ()))


def dot(a, b, dims=NN):
    return lax.dot_general(a, b, dims, preferred_element_type=F32)


def kernel(
    x_hbm, wv_hbm, wg_hbm, first_hbm, second_hbm, cot_hbm,
    mixed, gin, gf, gs_out,
    wv, wg, val, act, slope, part, first, second, tmp,
    send_a, send_b, cols_a, cols_b, send_c, send_d, rows_c, rows_d,
    gf_tmp, gf_own, gf_near, gf_near_in, gf_far, gf_far_in, gs,
    in_sem, f_send, f_recv, s_send, s_recv, ex_send, ex_recv, ex_own,
    near_send, near_recv, far_send, far_recv, gs_send, gs_recv, gs_own, group, ready,
):
    x, cot = mixed, gin
    width, length = lax.axis_size("dp"), lax.axis_size("seq")
    n = width * length
    traces, rows, columns, channels = x.shape
    mine = columns // n
    share = columns // width
    d, s = lax.axis_index("dp"), lax.axis_index("seq")
    me = s * width + d
    near = d + 1 - 2 * lax.rem(d, 2)
    far = lax.rem(d + 2, width)
    cross = lax.rem(near + 2, width)

    loads = [
        pltpu.make_async_copy(a, b, in_sem.at[i])
        for i, (a, b) in enumerate(
            [
                (x_hbm, x), (cot_hbm, cot), (wg_hbm, wg), (wv_hbm, wv),
                (first_hbm, first.at[:, pl.ds(pl.multiple_of(share * d, share), share), :]),
                (
                    second_hbm.at[pl.ds(mine * d, mine)],
                    second.at[:, pl.ds(pl.multiple_of(share * d, share), share), :],
                ),
            ]
        )
    ]
    for load in loads:
        load.start()

    barrier = pltpu.get_barrier_semaphore()

    def signal(sem, to_dp, to_seq):
        pl.semaphore_signal(sem, inc=1, device_id=(to_dp, to_seq), device_id_type=MESH)

    @pl.when(d != 0)
    def _():
        signal(barrier, 0, s)

    @pl.when(d == 0)
    def _():
        pl.semaphore_wait(barrier, width - 1)
        for other in range(1, width):
            signal(group, other, s)

    @pl.when(d != 0)
    def _():
        pl.semaphore_wait(group, 1)

    def remote(a, b, send, recv, to_dp, to_seq):
        return pltpu.make_async_remote_copy(
            a, b, send, recv, device_id=(to_dp, to_seq), device_id_type=MESH
        )

    def block(owner):
        return pl.ds(pl.multiple_of(share * owner, share), share)

    first_far = remote(first_hbm, first.at[:, block(d), :], f_send.at[0], f_recv.at[0], far, s)
    first_near = remote(first_hbm, first.at[:, block(d), :], f_send.at[1], f_recv.at[1], near, s)
    first_pass = remote(
        first.at[:, block(far), :], first.at[:, block(far), :], f_send.at[2], f_recv.at[2], near, s
    )
    first_far.start()
    first_near.start()

    def second_to(other):
        return remote(
            second_hbm.at[pl.ds(mine * other, mine)], second.at[:, block(d), :],
            s_send, s_recv, other, s,
        )

    for other in (far, cross, near):
        second_to(other).start()

    @pl.when(d == 1)
    def _():
        def greet(k, carry):
            signal(barrier, 1, lax.rem(s + k, length))
            return carry

        lax.fori_loop(1, length, greet, 0)

    def pieces_wait(sem):
        rest = send_a.at[:, pl.ds(0, columns - mine)]
        pltpu.make_async_copy(rest, rest, sem).wait()

    def to_columns(buf, out, which):
        def target(o):
            return o.at[pl.ds(traces * d, traces), :, pl.ds(pl.multiple_of(rows * s, rows), rows), :]

        own = pltpu.make_async_copy(
            buf.at[:, pl.ds(mine * me, mine)], target(out), ex_own.at[which]
        )
        own.start()

        def send(k, carry):
            e = lax.rem(me + k, n)
            remote(
                buf.at[:, pl.ds(mine * e, mine)], target(out),
                ex_send.at[which], ex_recv.at[which], lax.rem(e, width), e // width,
            ).start()
            return carry

        lax.fori_loop(1, n, send, 0)
        return own

    def source(buf, e_dp, e_seq):
        return buf.at[
            pl.ds(traces * e_dp, traces), :, pl.ds(pl.multiple_of(rows * e_seq, rows), rows), :
        ]

    def to_rows(buf, out, which, e_dp, first_k):
        def send(k, carry):
            e_seq = lax.rem(s + k, length)
            remote(
                source(buf, e_dp, e_seq), out.at[:, pl.ds(mine * me, mine)],
                ex_send.at[which], ex_recv.at[which], e_dp, e_seq,
            ).start()
            return carry

        lax.fori_loop(first_k, length, send, 0)

    step = 64

    def pack(buf):
        def body(i, carry):
            t, k = i // (columns // step), lax.rem(i, columns // step)
            rows_here = pl.ds(pl.multiple_of(k * step * rows, step * rows), step * rows)
            y = tmp[t, rows_here, :].reshape(step, rows, channels)
            buf[t, pl.ds(k * step, step)] = y.astype(BF)
            return carry

        lax.fori_loop(0, traces * (columns // step), body, 0)

    def unpack(buf):
        def body(i, carry):
            t, k = i // (columns // step), lax.rem(i, columns // step)
            rows_here = pl.ds(pl.multiple_of(k * step * rows, step * rows), step * rows)
            y = buf[t, pl.ds(k * step, step)].astype(F32)
            tmp[t, rows_here, :] = y.reshape(step * rows, channels)
            return carry

        lax.fori_loop(0, traces * (columns // step), body, 0)

    def row(p):
        return pl.ds(p, columns, stride=rows)

    loads[0].wait()
    loads[1].wait()
    loads[2].wait()

    def gate(i, carry):
        t, p = i // rows, lax.rem(i, rows)
        g = dot(x[t, p], wg[...])
        sig = jax.nn.sigmoid(g)
        a = g * sig
        c = cot[t, p].astype(F32)
        act[t, p] = a
        slope[t, p] = c * sig * (1.0 + g * (1.0 - sig))
        tmp[t, row(p), :] = c * a
        return carry

    lax.fori_loop(0, rows, gate, 0)

    @pl.when(d == 1)
    def _():
        pl.semaphore_wait(barrier, length - 1)
        for other in (0, *range(2, width)):
            signal(ready, other, s)

    lax.fori_loop(rows, traces * rows, gate, 0)
    pack(send_a)

    @pl.when(d != 1)
    def _():
        pl.semaphore_wait(ready, 1)

    own_a = to_columns(send_a, cols_a, 0)
    loads[3].wait()

    def value(i, carry):
        t, p = i // rows, lax.rem(i, rows)
        val[t, p] = dot(x[t, p], wv[...]).astype(BF)
        return carry

    lax.fori_loop(0, traces * rows, value, 0)

    loads[4].wait()
    first_far.wait_recv()
    first_pass.start()
    first_near.wait_recv()
    first_pass.wait_recv()

    def both(ref, p):
        return jnp.concatenate([ref[t, p] for t in range(traces)], axis=1)

    def mix_rows(p, carry):
        o = dot(first[p], both(val, p))
        for t in range(traces):
            tmp[t, row(p), :] = o[:, t * channels : (t + 1) * channels]
        return carry

    lax.fori_loop(0, rows, mix_rows, 0)
    pack(send_b)
    own_b = to_columns(send_b, cols_b, 1)

    loads[5].wait()
    half = second.at[:, pl.ds(0, share * (width - 1)), :]
    pltpu.make_async_copy(half, half, s_recv).wait()

    def columns_back(cols, buf, out, which, dims):
        owns = []
        for k in range(width):
            e_dp = lax.rem(d + k, width)

            def mix(q, carry):
                r = jnp.concatenate(
                    [cols[traces * e_dp + t, q] for t in range(traces)], axis=1
                )
                o = dot(second[q], r, dims).astype(BF)
                for t in range(traces):
                    buf[traces * e_dp + t, q] = o[:, t * channels : (t + 1) * channels]
                return carry

            lax.fori_loop(0, mine, mix, 0)
            if k == 0:
                own = pltpu.make_async_copy(
                    source(buf, d, s), out.at[:, pl.ds(mine * me, mine)], ex_own.at[which]
                )
                own.start()
                owns.append(own)
            to_rows(buf, out, which, e_dp, 1 if k == 0 else 0)
        return owns[0]

    own_a.wait()
    pieces_wait(ex_recv.at[0])
    own_c = columns_back(cols_a, send_c, rows_c, 2, TN)
    own_b.wait()
    pieces_wait(ex_recv.at[1])
    own_d = columns_back(cols_b, send_d, rows_d, 3, NN)

    scale = 1.0 / (traces * width)

    def second_grad(q, carry):
        a = jnp.concatenate([cols_a[t, q] for t in range(traces * width)], axis=1)
        b = jnp.concatenate([cols_b[t, q] for t in range(traces * width)], axis=1)
        gs[q] = (dot(a, b, NT) * scale).astype(BF)
        return carry

    lax.fori_loop(0, mine, second_grad, 0)

    def gs_to(other):
        return remote(
            gs.at[:, block(other), :], gs_out.at[pl.ds(mine * d, mine)], gs_send, gs_recv, other, s
        )

    gs_mine = pltpu.make_async_copy(gs.at[:, block(d), :], gs_out.at[pl.ds(mine * d, mine)], gs_own)
    gs_mine.start()
    for other in (far, cross, near):
        gs_to(other).start()

    own_c.wait()
    pieces_wait(ex_recv.at[2])
    unpack(rows_c)

    def near_copy(p):
        return remote(gf_near.at[p], gf_near_in.at[p], near_send.at[p], near_recv.at[p], near, s)

    def far_copy(p):
        return remote(gf_far.at[p], gf_far_in.at[p], far_send.at[p], far_recv.at[p], far, s)

    def rows_back(p, carry):
        r = jnp.concatenate([tmp[t, row(p), :] for t in range(traces)], axis=1).astype(BF)
        gf_tmp[...] = dot(r, both(val, p), NT)
        gf_own[p, 0] = gf_tmp[block(d), :]
        gf_own[p, 1] = gf_tmp[block(far), :]
        gf_near[p, 0] = gf_tmp[block(near), :].astype(BF)
        gf_near[p, 1] = gf_tmp[block(cross), :].astype(BF)
        near_copy(p).start()
        v = dot(first[p], r, TN).astype(BF)
        for t in range(traces):
            part[t, p] = dot(v[:, t * channels : (t + 1) * channels], wv[...], NT)
        return carry

    lax.fori_loop(0, rows, rows_back, 0)

    def reduce_near(p, carry):
        near_copy(p).wait_recv()
        gf_far[p] = (gf_own[p, 1] + gf_near_in[p, 1].astype(F32)).astype(BF)
        gf_own[p, 0] = gf_own[p, 0] + gf_near_in[p, 0].astype(F32)
        return carry

    lax.fori_loop(0, rows, reduce_near, 0)

    def send_far(p, carry):
        far_copy(p).start()
        return carry

    lax.fori_loop(0, rows // 2, send_far, 0)

    own_d.wait()
    pieces_wait(ex_recv.at[3])
    lax.fori_loop(rows // 2, rows, send_far, 0)
    unpack(rows_d)

    def finish(i, carry):
        t, p = i // rows, lax.rem(i, rows)
        c = tmp[t, row(p), :]
        mixed[t, p] = (c * act[t, p]).astype(BF)
        g = (c * slope[t, p]).astype(BF)
        gin[t, p] = (part[t, p] + dot(g, wg[...], NT)).astype(BF)
        return carry

    lax.fori_loop(0, traces * rows, finish, 0)

    def reduce_far(p, carry):
        far_copy(p).wait_recv()
        gf[p] = ((gf_own[p, 0] + gf_far_in[p].astype(F32)) * scale).astype(BF)
        return carry

    lax.fori_loop(0, rows, reduce_far, 0)

    first_far.wait_send()
    first_near.wait_send()
    first_pass.wait_send()
    pltpu.make_async_copy(half, half, s_send).wait()
    for which in range(4):
        pieces_wait(ex_send.at[which])

    def sent(p, carry):
        far_copy(p).wait_send()
        near_copy(p).wait_send()
        return carry

    lax.fori_loop(0, rows, sent, 0)
    gs_mine.wait()
    three = gs.at[:, pl.ds(0, share * (width - 1)), :]
    pltpu.make_async_copy(three, three, gs_send).wait()
    pltpu.make_async_copy(three, three, gs_recv).wait()


def write_kernel(*refs):
    sem = refs[-1]
    half = len(refs) // 2
    copies = [
        pltpu.make_async_copy(a, b, sem.at[i]) for i, (a, b) in enumerate(zip(refs[:half], refs[half:-1]))
    ]
    for copy in copies:
        copy.start()
    for copy in copies:
        copy.wait()


def on_device(traces_in, w_value, w_gate, first_blocks, second_blocks, cotangent):
    width, length = lax.axis_size("dp"), lax.axis_size("seq")
    traces, rows, columns, channels = traces_in.shape
    mine, share = columns // (width * length), columns // width
    by_row = (traces, columns, rows, channels)
    by_column = (traces * width, mine, rows * length, channels)
    hbm = pl.BlockSpec(memory_space=pl.ANY)
    dma = pltpu.SemaphoreType.DMA
    V = pltpu.VMEM
    shape = traces_in.shape
    vmem = pl.BlockSpec(memory_space=pltpu.VMEM)
    out_shape = [
        jax.ShapeDtypeStruct(shape, BF),
        jax.ShapeDtypeStruct(shape, BF),
        jax.ShapeDtypeStruct(first_blocks.shape, BF),
        jax.ShapeDtypeStruct(second_blocks.shape, BF),
    ]
    outs = pl.pallas_call(
        kernel,
        out_shape=[pltpu.VMEM(o.shape, o.dtype) for o in out_shape],
        in_specs=[hbm] * 6,
        out_specs=[vmem] * 4,
        scratch_shapes=[
            V(w_value.shape, BF), V(w_gate.shape, BF), V(shape, BF),
            V(shape, F32), V(shape, F32), V(shape, F32),
            V((rows, columns, columns), BF), V((mine, columns, columns), BF),
            V((traces, columns * rows, channels), F32),
            V(by_row, BF), V(by_row, BF), V(by_column, BF), V(by_column, BF),
            V(by_column, BF), V(by_column, BF), V(by_row, BF), V(by_row, BF),
            V((columns, columns), F32), V((rows, 2, share, columns), F32),
            V((rows, 2, share, columns), BF), V((rows, 2, share, columns), BF),
            V((rows, share, columns), BF), V((rows, share, columns), BF),
            V((mine, columns, columns), BF),
            dma((6,)), dma((3,)), dma((3,)), dma, dma, dma((4,)), dma((4,)), dma((4,)),
            dma((rows,)), dma((rows,)), dma((rows,)), dma((rows,)), dma, dma, dma,
            pltpu.SemaphoreType.REGULAR, pltpu.SemaphoreType.REGULAR,
        ],
        compiler_params=pltpu.CompilerParams(
            collective_id=1, has_side_effects=True, vmem_limit_bytes=52 << 20
        ),
    )(traces_in, w_value, w_gate, first_blocks, second_blocks, cotangent)
    return pl.pallas_call(
        write_kernel,
        out_shape=out_shape,
        in_specs=[vmem] * 4,
        out_specs=[hbm] * 4,
        scratch_shapes=[dma((4,))],
        compiler_params=pltpu.CompilerParams(vmem_limit_bytes=8 << 20),
    )(*[pltpu.with_memory_space_constraint(o, pltpu.VMEM) for o in outs])


def solution(mesh):
    big, weight = P("dp", "seq", None, None), P("seq", "dp", None)
    return jax.shard_map(
        on_device,
        mesh=mesh,
        in_specs=(big, P(), P(), weight, weight, big),
        out_specs=(big, big, weight, weight),
        check_vma=False,
    )
```

```python
import jax
import jax.numpy as jnp
from jax import lax
from jax.experimental import pallas as pl
from jax.experimental.pallas import tpu as pltpu
from jax.sharding import PartitionSpec as P

MESH = pl.DeviceIdType.MESH
BF = jnp.bfloat16
F32 = jnp.float32
NT = (((1,), (1,)), ((), ()))
TN = (((0,), (0,)), ((), ()))
NN = (((1,), (0,)), ((), ()))


def dot(a, b, dims=NN):
    return lax.dot_general(a, b, dims, preferred_element_type=F32)


def kernel(
    x_hbm, wv_hbm, wg_hbm, first_hbm, second_hbm, cot_hbm,
    mixed, gin, gf, gs_out,
    wv, wg, val, act, slope, part, first, second, tmp,
    send_a, send_b, cols_a, cols_b, send_c, send_d, rows_c, rows_d,
    gf_tmp, gf_own, gf_near, gf_near_in, gf_far, gf_far_in, gs,
    in_sem, f_send, f_recv, s_send, s_recv, ex_send, ex_recv, ex_own,
    near_send, near_recv, far_send, far_recv, gs_send, gs_recv, gs_own, group, ready,
):
    x, cot = mixed, gin
    width, length = lax.axis_size("dp"), lax.axis_size("seq")
    n = width * length
    traces, rows, columns, channels = x.shape
    mine = columns // n
    share = columns // width
    d, s = lax.axis_index("dp"), lax.axis_index("seq")
    me = s * width + d
    near = d + 1 - 2 * lax.rem(d, 2)
    far = lax.rem(d + 2, width)
    cross = lax.rem(near + 2, width)

    loads = [
        pltpu.make_async_copy(a, b, in_sem.at[i])
        for i, (a, b) in enumerate(
            [
                (x_hbm, x), (cot_hbm, cot), (wg_hbm, wg), (wv_hbm, wv),
                (first_hbm, first.at[:, pl.ds(pl.multiple_of(share * d, share), share), :]),
                (
                    second_hbm.at[pl.ds(mine * d, mine)],
                    second.at[:, pl.ds(pl.multiple_of(share * d, share), share), :],
                ),
            ]
        )
    ]
    barrier = pltpu.get_barrier_semaphore()

    def signal(sem, to_dp, to_seq):
        pl.semaphore_signal(sem, inc=1, device_id=(to_dp, to_seq), device_id_type=MESH)

    for other in (0, *range(2, width)):

        @pl.when(d != other)
        def _(other=other):
            signal(barrier, other, s)

    for load in loads:
        load.start()

    @pl.when(d != 1)
    def _():
        pl.semaphore_wait(barrier, width - 1)

    @pl.when(d == 0)
    def _():
        signal(group, 1, s)

    @pl.when(d == 1)
    def _():
        pl.semaphore_wait(group, 1)

    def remote(a, b, send, recv, to_dp, to_seq):
        return pltpu.make_async_remote_copy(
            a, b, send, recv, device_id=(to_dp, to_seq), device_id_type=MESH
        )

    def block(owner):
        return pl.ds(pl.multiple_of(share * owner, share), share)

    first_far = remote(first_hbm, first.at[:, block(d), :], f_send.at[0], f_recv.at[0], far, s)
    first_near = remote(first_hbm, first.at[:, block(d), :], f_send.at[1], f_recv.at[1], near, s)
    first_pass = remote(
        first.at[:, block(far), :], first.at[:, block(far), :], f_send.at[2], f_recv.at[2], near, s
    )
    first_far.start()
    first_near.start()

    def second_to(other):
        return remote(
            second_hbm.at[pl.ds(mine * other, mine)], second.at[:, block(d), :],
            s_send, s_recv, other, s,
        )

    for other in (far, cross, near):
        second_to(other).start()

    @pl.when(d == 1)
    def _():
        def greet(k, carry):
            signal(barrier, 1, lax.rem(s + k, length))
            return carry

        lax.fori_loop(1, length, greet, 0)

    def pieces_wait(sem):
        rest = send_a.at[:, pl.ds(0, columns - mine)]
        pltpu.make_async_copy(rest, rest, sem).wait()

    def to_columns(buf, out, which):
        def target(o):
            return o.at[pl.ds(traces * d, traces), :, pl.ds(pl.multiple_of(rows * s, rows), rows), :]

        own = pltpu.make_async_copy(
            buf.at[:, pl.ds(mine * me, mine)], target(out), ex_own.at[which]
        )
        own.start()

        def send(k, carry):
            e = lax.rem(me + k, n)
            remote(
                buf.at[:, pl.ds(mine * e, mine)], target(out),
                ex_send.at[which], ex_recv.at[which], lax.rem(e, width), e // width,
            ).start()
            return carry

        lax.fori_loop(1, n, send, 0)
        return own

    def source(buf, e_dp, e_seq):
        return buf.at[
            pl.ds(traces * e_dp, traces), :, pl.ds(pl.multiple_of(rows * e_seq, rows), rows), :
        ]

    def to_rows(buf, out, which, e_dp, first_k):
        def send(k, carry):
            e_seq = lax.rem(s + k, length)
            remote(
                source(buf, e_dp, e_seq), out.at[:, pl.ds(mine * me, mine)],
                ex_send.at[which], ex_recv.at[which], e_dp, e_seq,
            ).start()
            return carry

        lax.fori_loop(first_k, length, send, 0)

    step = 64

    def pack(buf):
        def body(i, carry):
            t, k = i // (columns // step), lax.rem(i, columns // step)
            rows_here = pl.ds(pl.multiple_of(k * step * rows, step * rows), step * rows)
            y = tmp[t, rows_here, :].reshape(step, rows, channels)
            buf[t, pl.ds(k * step, step)] = y.astype(BF)
            return carry

        lax.fori_loop(0, traces * (columns // step), body, 0)

    def unpack(buf):
        def body(i, carry):
            t, k = i // (columns // step), lax.rem(i, columns // step)
            rows_here = pl.ds(pl.multiple_of(k * step * rows, step * rows), step * rows)
            y = buf[t, pl.ds(k * step, step)].astype(F32)
            tmp[t, rows_here, :] = y.reshape(step * rows, channels)
            return carry

        lax.fori_loop(0, traces * (columns // step), body, 0)

    def row(p):
        return pl.ds(p, columns, stride=rows)

    loads[0].wait()
    loads[1].wait()
    loads[2].wait()

    def gate(i, carry):
        t, p = i // rows, lax.rem(i, rows)
        g = dot(x[t, p], wg[...])
        sig = jax.nn.sigmoid(g)
        a = g * sig
        c = cot[t, p].astype(F32)
        act[t, p] = a
        slope[t, p] = c * sig * (1.0 + g * (1.0 - sig))
        tmp[t, row(p), :] = c * a
        return carry

    lax.fori_loop(0, rows, gate, 0)

    @pl.when(d == 1)
    def _():
        pl.semaphore_wait(barrier, length - 1)
        for other in (0, *range(2, width)):
            signal(ready, other, s)

    lax.fori_loop(rows, traces * rows, gate, 0)
    pack(send_a)

    @pl.when(d != 1)
    def _():
        pl.semaphore_wait(ready, 1)

    own_a = to_columns(send_a, cols_a, 0)
    loads[3].wait()

    def value(i, carry):
        t, p = i // rows, lax.rem(i, rows)
        val[t, p] = dot(x[t, p], wv[...]).astype(BF)
        return carry

    lax.fori_loop(0, traces * rows, value, 0)

    loads[4].wait()
    first_far.wait_recv()
    first_pass.start()
    first_near.wait_recv()
    first_pass.wait_recv()

    def both(ref, p):
        return jnp.concatenate([ref[t, p] for t in range(traces)], axis=1)

    def mix_rows(p, carry):
        o = dot(first[p], both(val, p))
        for t in range(traces):
            tmp[t, row(p), :] = o[:, t * channels : (t + 1) * channels]
        return carry

    lax.fori_loop(0, rows, mix_rows, 0)
    pack(send_b)
    own_b = to_columns(send_b, cols_b, 1)

    loads[5].wait()
    half = second.at[:, pl.ds(0, share * (width - 1)), :]
    pltpu.make_async_copy(half, half, s_recv).wait()

    def columns_back(cols, buf, out, which, dims):
        owns = []
        for k in range(width):
            e_dp = lax.rem(d + k, width)

            def mix(q, carry):
                r = jnp.concatenate(
                    [cols[traces * e_dp + t, q] for t in range(traces)], axis=1
                )
                o = dot(second[q], r, dims).astype(BF)
                for t in range(traces):
                    buf[traces * e_dp + t, q] = o[:, t * channels : (t + 1) * channels]
                return carry

            lax.fori_loop(0, mine, mix, 0)
            if k == 0:
                own = pltpu.make_async_copy(
                    source(buf, d, s), out.at[:, pl.ds(mine * me, mine)], ex_own.at[which]
                )
                own.start()
                owns.append(own)
            to_rows(buf, out, which, e_dp, 1 if k == 0 else 0)
        return owns[0]

    own_a.wait()
    pieces_wait(ex_recv.at[0])
    own_c = columns_back(cols_a, send_c, rows_c, 2, TN)
    own_b.wait()
    pieces_wait(ex_recv.at[1])
    own_d = columns_back(cols_b, send_d, rows_d, 3, NN)

    scale = 1.0 / (traces * width)

    def second_grad(q, carry):
        a = jnp.concatenate([cols_a[t, q] for t in range(traces * width)], axis=1)
        b = jnp.concatenate([cols_b[t, q] for t in range(traces * width)], axis=1)
        gs[q] = (dot(a, b, NT) * scale).astype(BF)
        return carry

    lax.fori_loop(0, mine, second_grad, 0)

    def gs_to(other):
        return remote(
            gs.at[:, block(other), :], gs_out.at[pl.ds(mine * d, mine)], gs_send, gs_recv, other, s
        )

    gs_mine = pltpu.make_async_copy(gs.at[:, block(d), :], gs_out.at[pl.ds(mine * d, mine)], gs_own)
    gs_mine.start()
    for other in (far, cross, near):
        gs_to(other).start()

    own_c.wait()
    pieces_wait(ex_recv.at[2])
    unpack(rows_c)

    def near_copy(p):
        return remote(gf_near.at[p], gf_near_in.at[p], near_send.at[p], near_recv.at[p], near, s)

    def far_copy(p):
        return remote(gf_far.at[p], gf_far_in.at[p], far_send.at[p], far_recv.at[p], far, s)

    def rows_back(p, carry):
        r = jnp.concatenate([tmp[t, row(p), :] for t in range(traces)], axis=1).astype(BF)
        gf_tmp[...] = dot(r, both(val, p), NT)
        gf_own[p, 0] = gf_tmp[block(d), :]
        gf_own[p, 1] = gf_tmp[block(far), :]
        gf_near[p, 0] = gf_tmp[block(near), :].astype(BF)
        gf_near[p, 1] = gf_tmp[block(cross), :].astype(BF)
        near_copy(p).start()
        v = dot(first[p], r, TN).astype(BF)
        for t in range(traces):
            part[t, p] = dot(v[:, t * channels : (t + 1) * channels], wv[...], NT)
        return carry

    lax.fori_loop(0, rows, rows_back, 0)

    def reduce_near(p, carry):
        near_copy(p).wait_recv()
        gf_far[p] = (gf_own[p, 1] + gf_near_in[p, 1].astype(F32)).astype(BF)
        gf_own[p, 0] = gf_own[p, 0] + gf_near_in[p, 0].astype(F32)
        return carry

    lax.fori_loop(0, rows, reduce_near, 0)

    def send_far(p, carry):
        far_copy(p).start()
        return carry

    lax.fori_loop(0, rows // 2, send_far, 0)

    own_d.wait()
    pieces_wait(ex_recv.at[3])
    lax.fori_loop(rows // 2, rows, send_far, 0)
    unpack(rows_d)

    def finish(i, carry):
        t, p = i // rows, lax.rem(i, rows)
        c = tmp[t, row(p), :]
        mixed[t, p] = (c * act[t, p]).astype(BF)
        g = (c * slope[t, p]).astype(BF)
        gin[t, p] = (part[t, p] + dot(g, wg[...], NT)).astype(BF)
        return carry

    lax.fori_loop(0, traces * rows, finish, 0)

    first_far.wait_send()
    first_near.wait_send()
    first_pass.wait_send()
    pltpu.make_async_copy(half, half, s_send).wait()
    for which in range(4):
        pieces_wait(ex_send.at[which])

    gs_mine.wait()
    three = gs.at[:, pl.ds(0, share * (width - 1)), :]
    pltpu.make_async_copy(three, three, gs_send).wait()
    pltpu.make_async_copy(three, three, gs_recv).wait()

    def near_sent(p, carry):
        near_copy(p).wait_send()
        return carry

    lax.fori_loop(0, rows, near_sent, 0)

    def reduce_far(p, carry):
        far_copy(p).wait_recv()
        gf[p] = ((gf_own[p, 0] + gf_far_in[p].astype(F32)) * scale).astype(BF)
        return carry

    lax.fori_loop(0, rows, reduce_far, 0)

    def sent(p, carry):
        far_copy(p).wait_send()
        return carry

    lax.fori_loop(0, rows, sent, 0)


def write_kernel(*refs):
    sem = refs[-1]
    half = len(refs) // 2
    copies = []
    for a, b in zip(refs[:half], refs[half:-1]):
        cut = a.shape[0] // 2
        for part in (pl.ds(0, cut), pl.ds(cut, cut)):
            copies.append(pltpu.make_async_copy(a.at[part], b.at[part], sem.at[len(copies)]))
    for copy in copies:
        copy.start()
    for copy in copies:
        copy.wait()


def on_device(traces_in, w_value, w_gate, first_blocks, second_blocks, cotangent):
    width, length = lax.axis_size("dp"), lax.axis_size("seq")
    traces, rows, columns, channels = traces_in.shape
    mine, share = columns // (width * length), columns // width
    by_row = (traces, columns, rows, channels)
    by_column = (traces * width, mine, rows * length, channels)
    hbm = pl.BlockSpec(memory_space=pl.ANY)
    dma = pltpu.SemaphoreType.DMA
    V = pltpu.VMEM
    shape = traces_in.shape
    vmem = pl.BlockSpec(memory_space=pltpu.VMEM)
    out_shape = [
        jax.ShapeDtypeStruct(shape, BF),
        jax.ShapeDtypeStruct(shape, BF),
        jax.ShapeDtypeStruct(first_blocks.shape, BF),
        jax.ShapeDtypeStruct(second_blocks.shape, BF),
    ]
    outs = pl.pallas_call(
        kernel,
        out_shape=[pltpu.VMEM(o.shape, o.dtype) for o in out_shape],
        in_specs=[hbm] * 6,
        out_specs=[vmem] * 4,
        scratch_shapes=[
            V(w_value.shape, BF), V(w_gate.shape, BF), V(shape, BF),
            V(shape, F32), V(shape, F32), V(shape, F32),
            V((rows, columns, columns), BF), V((mine, columns, columns), BF),
            V((traces, columns * rows, channels), F32),
            V(by_row, BF), V(by_row, BF), V(by_column, BF), V(by_column, BF),
            V(by_column, BF), V(by_column, BF), V(by_row, BF), V(by_row, BF),
            V((columns, columns), F32), V((rows, 2, share, columns), F32),
            V((rows, 2, share, columns), BF), V((rows, 2, share, columns), BF),
            V((rows, share, columns), BF), V((rows, share, columns), BF),
            V((mine, columns, columns), BF),
            dma((6,)), dma((3,)), dma((3,)), dma, dma, dma((4,)), dma((4,)), dma((4,)),
            dma((rows,)), dma((rows,)), dma((rows,)), dma((rows,)), dma, dma, dma,
            pltpu.SemaphoreType.REGULAR, pltpu.SemaphoreType.REGULAR,
        ],
        compiler_params=pltpu.CompilerParams(
            collective_id=1, has_side_effects=True, vmem_limit_bytes=52 << 20
        ),
    )(traces_in, w_value, w_gate, first_blocks, second_blocks, cotangent)
    return pl.pallas_call(
        write_kernel,
        out_shape=out_shape,
        in_specs=[vmem] * 4,
        out_specs=[hbm] * 4,
        scratch_shapes=[dma((8,))],
        compiler_params=pltpu.CompilerParams(vmem_limit_bytes=8 << 20),
    )(*[pltpu.with_memory_space_constraint(o, pltpu.VMEM) for o in outs])


def solution(mesh):
    big, weight = P("dp", "seq", None, None), P("seq", "dp", None)
    return jax.shard_map(
        on_device,
        mesh=mesh,
        in_specs=(big, P(), P(), weight, weight, big),
        out_specs=(big, big, weight, weight),
        check_vma=False,
    )
```

```python
import jax
import jax.numpy as jnp
from jax import lax
from jax.experimental import pallas as pl
from jax.experimental.pallas import tpu as pltpu
from jax.sharding import PartitionSpec as P

MESH = pl.DeviceIdType.MESH
BF = jnp.bfloat16
F32 = jnp.float32
NT = (((1,), (1,)), ((), ()))
TN = (((0,), (0,)), ((), ()))
NN = (((1,), (0,)), ((), ()))


def dot(a, b, dims=NN):
    return lax.dot_general(a, b, dims, preferred_element_type=F32)


def kernel(
    x_hbm, wv_hbm, wg_hbm, first_hbm, second_hbm, cot_hbm,
    mixed, gin, gf, gs_out,
    wv, wg, val, act, slope, part, first, second, tmp,
    send_a, send_b, cols_a, cols_b, send_c, send_d, rows_c, rows_d,
    gf_tmp, gf_own, gf_near, gf_near_in, gf_far, gf_far_in, gs,
    in_sem, f_send, f_recv, s_send, s_recv, ex_send, ex_recv, ex_own,
    near_send, near_recv, far_send, far_recv, gs_send, gs_recv, gs_own, group, ready,
):
    x, cot = mixed, gin
    width, length = lax.axis_size("dp"), lax.axis_size("seq")
    n = width * length
    traces, rows, columns, channels = x.shape
    mine = columns // n
    share = columns // width
    d, s = lax.axis_index("dp"), lax.axis_index("seq")
    me = s * width + d
    near = d + 1 - 2 * lax.rem(d, 2)
    far = lax.rem(d + 2, width)
    cross = lax.rem(near + 2, width)

    loads = [
        pltpu.make_async_copy(a, b, in_sem.at[i])
        for i, (a, b) in enumerate(
            [
                (x_hbm, x), (cot_hbm, cot), (wg_hbm, wg), (wv_hbm, wv),
                (first_hbm, first.at[:, pl.ds(pl.multiple_of(share * d, share), share), :]),
                (
                    second_hbm.at[pl.ds(mine * d, mine)],
                    second.at[:, pl.ds(pl.multiple_of(share * d, share), share), :],
                ),
            ]
        )
    ]
    for load in loads:
        load.start()

    barrier = pltpu.get_barrier_semaphore()

    def signal(sem, to_dp, to_seq):
        pl.semaphore_signal(sem, inc=1, device_id=(to_dp, to_seq), device_id_type=MESH)

    @pl.when(d != 0)
    def _():
        signal(barrier, 0, s)

    @pl.when(d == 0)
    def _():
        pl.semaphore_wait(barrier, width - 1)
        for other in range(1, width):
            signal(group, other, s)

    @pl.when(d != 0)
    def _():
        pl.semaphore_wait(group, 1)

    def remote(a, b, send, recv, to_dp, to_seq):
        return pltpu.make_async_remote_copy(
            a, b, send, recv, device_id=(to_dp, to_seq), device_id_type=MESH
        )

    def block(owner):
        return pl.ds(pl.multiple_of(share * owner, share), share)

    first_far = remote(first_hbm, first.at[:, block(d), :], f_send.at[0], f_recv.at[0], far, s)
    first_near = remote(first_hbm, first.at[:, block(d), :], f_send.at[1], f_recv.at[1], near, s)
    first_pass = remote(
        first.at[:, block(far), :], first.at[:, block(far), :], f_send.at[2], f_recv.at[2], near, s
    )
    first_far.start()
    first_near.start()

    def second_to(other):
        return remote(
            second_hbm.at[pl.ds(mine * other, mine)], second.at[:, block(d), :],
            s_send, s_recv, other, s,
        )

    for other in (far, cross, near):
        second_to(other).start()

    @pl.when(d == 1)
    def _():
        def greet(k, carry):
            signal(barrier, 1, lax.rem(s + k, length))
            return carry

        lax.fori_loop(1, length, greet, 0)

    def pieces_wait(sem):
        rest = send_a.at[:, pl.ds(0, columns - mine)]
        pltpu.make_async_copy(rest, rest, sem).wait()

    def to_columns(buf, out, which):
        def target(o):
            return o.at[pl.ds(traces * d, traces), :, pl.ds(pl.multiple_of(rows * s, rows), rows), :]

        own = pltpu.make_async_copy(
            buf.at[:, pl.ds(mine * me, mine)], target(out), ex_own.at[which]
        )
        own.start()

        def send(k, carry):
            e = lax.rem(me + k, n)
            remote(
                buf.at[:, pl.ds(mine * e, mine)], target(out),
                ex_send.at[which], ex_recv.at[which], lax.rem(e, width), e // width,
            ).start()
            return carry

        lax.fori_loop(1, n, send, 0)
        return own

    def source(buf, e_dp, e_seq):
        return buf.at[
            pl.ds(traces * e_dp, traces), :, pl.ds(pl.multiple_of(rows * e_seq, rows), rows), :
        ]

    def to_rows(buf, out, which, came, e_dp, first_k):
        def send(k, carry):
            e_seq = lax.rem(s + k, length)
            remote(
                source(buf, e_dp, e_seq), out.at[:, pl.ds(mine * me, mine)],
                ex_send.at[which], ex_recv.at[came], e_dp, e_seq,
            ).start()
            return carry

        lax.fori_loop(first_k, length, send, 0)

    step = 64

    def pack(buf):
        def body(i, carry):
            t, k = i // (columns // step), lax.rem(i, columns // step)
            rows_here = pl.ds(pl.multiple_of(k * step * rows, step * rows), step * rows)
            y = tmp[t, rows_here, :].reshape(step, rows, channels)
            buf[t, pl.ds(k * step, step)] = y.astype(BF)
            return carry

        lax.fori_loop(0, traces * (columns // step), body, 0)

    def unpack(buf):
        def body(i, carry):
            t, k = i // (columns // step), lax.rem(i, columns // step)
            rows_here = pl.ds(pl.multiple_of(k * step * rows, step * rows), step * rows)
            y = buf[t, pl.ds(k * step, step)].astype(F32)
            tmp[t, rows_here, :] = y.reshape(step * rows, channels)
            return carry

        lax.fori_loop(0, traces * (columns // step), body, 0)

    def row(p):
        return pl.ds(p, columns, stride=rows)

    loads[0].wait()
    loads[1].wait()
    loads[2].wait()

    def gate(i, carry):
        t, p = i // rows, lax.rem(i, rows)
        g = dot(x[t, p], wg[...])
        sig = jax.nn.sigmoid(g)
        a = g * sig
        c = cot[t, p].astype(F32)
        act[t, p] = a
        slope[t, p] = c * sig * (1.0 + g * (1.0 - sig))
        tmp[t, row(p), :] = c * a
        return carry

    lax.fori_loop(0, rows, gate, 0)

    @pl.when(d == 1)
    def _():
        pl.semaphore_wait(barrier, length - 1)
        for other in (0, *range(2, width)):
            signal(ready, other, s)

    lax.fori_loop(rows, traces * rows, gate, 0)
    pack(send_a)

    @pl.when(d != 1)
    def _():
        pl.semaphore_wait(ready, 1)

    own_a = to_columns(send_a, cols_a, 0)
    loads[3].wait()

    def value(i, carry):
        t, p = i // rows, lax.rem(i, rows)
        val[t, p] = dot(x[t, p], wv[...]).astype(BF)
        return carry

    lax.fori_loop(0, traces * rows, value, 0)

    loads[4].wait()
    first_far.wait_recv()
    first_pass.start()
    first_near.wait_recv()
    first_pass.wait_recv()

    def both(ref, p):
        return jnp.concatenate([ref[t, p] for t in range(traces)], axis=1)

    def mix_rows(p, carry):
        o = dot(first[p], both(val, p))
        for t in range(traces):
            tmp[t, row(p), :] = o[:, t * channels : (t + 1) * channels]
        return carry

    lax.fori_loop(0, rows, mix_rows, 0)
    pack(send_b)
    own_b = to_columns(send_b, cols_b, 1)

    loads[5].wait()
    half = second.at[:, pl.ds(0, share * (width - 1)), :]
    pltpu.make_async_copy(half, half, s_recv).wait()

    def columns_back(cols, buf, out, which, dims, apart):
        owns = []
        for k in range(width):
            e_dp = lax.rem(d + k, width)

            def mix(q, carry):
                r = jnp.concatenate(
                    [cols[traces * e_dp + t, q] for t in range(traces)], axis=1
                )
                o = dot(second[q], r, dims).astype(BF)
                for t in range(traces):
                    buf[traces * e_dp + t, q] = o[:, t * channels : (t + 1) * channels]
                return carry

            lax.fori_loop(0, mine, mix, 0)
            if k == 0:
                own = pltpu.make_async_copy(
                    source(buf, d, s), out.at[:, pl.ds(mine * me, mine)], ex_own.at[which]
                )
                own.start()
                owns.append(own)
            came = which + k if apart else which
            to_rows(buf, out, which, came, e_dp, 1 if k == 0 else 0)
        return owns[0]

    own_a.wait()
    pieces_wait(ex_recv.at[0])
    own_c = columns_back(cols_a, send_c, rows_c, 2, TN, False)
    own_b.wait()
    pieces_wait(ex_recv.at[1])
    own_d = columns_back(cols_b, send_d, rows_d, 3, NN, True)

    scale = 1.0 / (traces * width)

    def second_grad(q, carry):
        a = jnp.concatenate([cols_a[t, q] for t in range(traces * width)], axis=1)
        b = jnp.concatenate([cols_b[t, q] for t in range(traces * width)], axis=1)
        gs[q] = (dot(a, b, NT) * scale).astype(BF)
        return carry

    lax.fori_loop(0, mine, second_grad, 0)

    def gs_to(other):
        return remote(
            gs.at[:, block(other), :], gs_out.at[pl.ds(mine * d, mine)], gs_send, gs_recv, other, s
        )

    gs_mine = pltpu.make_async_copy(gs.at[:, block(d), :], gs_out.at[pl.ds(mine * d, mine)], gs_own)
    gs_mine.start()
    for other in (far, cross, near):
        gs_to(other).start()

    own_c.wait()
    pieces_wait(ex_recv.at[2])
    unpack(rows_c)

    def near_copy(p):
        return remote(gf_near.at[p], gf_near_in.at[p], near_send.at[p], near_recv.at[p], near, s)

    def far_copy(p):
        return remote(gf_far.at[p], gf_far_in.at[p], far_send.at[p], far_recv.at[p], far, s)

    def rows_back(p, carry):
        r = jnp.concatenate([tmp[t, row(p), :] for t in range(traces)], axis=1).astype(BF)
        gf_tmp[...] = dot(r, both(val, p), NT)
        gf_own[p, 0] = gf_tmp[block(d), :]
        gf_own[p, 1] = gf_tmp[block(far), :]
        gf_near[p, 0] = gf_tmp[block(near), :].astype(BF)
        gf_near[p, 1] = gf_tmp[block(cross), :].astype(BF)
        near_copy(p).start()
        v = dot(first[p], r, TN).astype(BF)
        for t in range(traces):
            part[t, p] = dot(v[:, t * channels : (t + 1) * channels], wv[...], NT)
        return carry

    lax.fori_loop(0, rows, rows_back, 0)

    def reduce_near(p, carry):
        near_copy(p).wait_recv()
        gf_far[p] = (gf_own[p, 1] + gf_near_in[p, 1].astype(F32)).astype(BF)
        gf_own[p, 0] = gf_own[p, 0] + gf_near_in[p, 0].astype(F32)
        return carry

    lax.fori_loop(0, rows, reduce_near, 0)

    def send_far(p, carry):
        far_copy(p).start()
        return carry

    lax.fori_loop(0, rows // 2, send_far, 0)

    own_d.wait()

    def portion_wait(k):
        some = send_a.at[:, pl.ds(0, mine * (length - (1 if k == 0 else 0)))]
        pltpu.make_async_copy(some, some, ex_recv.at[3 + k]).wait()

    for k in range(width - 1):
        portion_wait(k)
    lax.fori_loop(rows // 2, rows, send_far, 0)
    portion_wait(width - 1)
    unpack(rows_d)

    def finish(i, carry):
        t, p = i // rows, lax.rem(i, rows)
        c = tmp[t, row(p), :]
        mixed[t, p] = (c * act[t, p]).astype(BF)
        g = (c * slope[t, p]).astype(BF)
        gin[t, p] = (part[t, p] + dot(g, wg[...], NT)).astype(BF)
        return carry

    lax.fori_loop(0, traces * rows, finish, 0)

    def reduce_far(p, carry):
        far_copy(p).wait_recv()
        gf[p] = ((gf_own[p, 0] + gf_far_in[p].astype(F32)) * scale).astype(BF)
        return carry

    lax.fori_loop(0, rows, reduce_far, 0)

    first_far.wait_send()
    first_near.wait_send()
    first_pass.wait_send()
    pltpu.make_async_copy(half, half, s_send).wait()
    for which in range(4):
        pieces_wait(ex_send.at[which])

    def sent(p, carry):
        far_copy(p).wait_send()
        near_copy(p).wait_send()
        return carry

    lax.fori_loop(0, rows, sent, 0)
    gs_mine.wait()
    three = gs.at[:, pl.ds(0, share * (width - 1)), :]
    pltpu.make_async_copy(three, three, gs_send).wait()
    pltpu.make_async_copy(three, three, gs_recv).wait()


def write_kernel(*refs):
    sem = refs[-1]
    half = len(refs) // 2
    copies = [
        pltpu.make_async_copy(a, b, sem.at[i]) for i, (a, b) in enumerate(zip(refs[:half], refs[half:-1]))
    ]
    for copy in copies:
        copy.start()
    for copy in copies:
        copy.wait()


def on_device(traces_in, w_value, w_gate, first_blocks, second_blocks, cotangent):
    width, length = lax.axis_size("dp"), lax.axis_size("seq")
    traces, rows, columns, channels = traces_in.shape
    mine, share = columns // (width * length), columns // width
    by_row = (traces, columns, rows, channels)
    by_column = (traces * width, mine, rows * length, channels)
    hbm = pl.BlockSpec(memory_space=pl.ANY)
    dma = pltpu.SemaphoreType.DMA
    V = pltpu.VMEM
    shape = traces_in.shape
    vmem = pl.BlockSpec(memory_space=pltpu.VMEM)
    out_shape = [
        jax.ShapeDtypeStruct(shape, BF),
        jax.ShapeDtypeStruct(shape, BF),
        jax.ShapeDtypeStruct(first_blocks.shape, BF),
        jax.ShapeDtypeStruct(second_blocks.shape, BF),
    ]
    outs = pl.pallas_call(
        kernel,
        out_shape=[pltpu.VMEM(o.shape, o.dtype) for o in out_shape],
        in_specs=[hbm] * 6,
        out_specs=[vmem] * 4,
        scratch_shapes=[
            V(w_value.shape, BF), V(w_gate.shape, BF), V(shape, BF),
            V(shape, F32), V(shape, F32), V(shape, F32),
            V((rows, columns, columns), BF), V((mine, columns, columns), BF),
            V((traces, columns * rows, channels), F32),
            V(by_row, BF), V(by_row, BF), V(by_column, BF), V(by_column, BF),
            V(by_column, BF), V(by_column, BF), V(by_row, BF), V(by_row, BF),
            V((columns, columns), F32), V((rows, 2, share, columns), F32),
            V((rows, 2, share, columns), BF), V((rows, 2, share, columns), BF),
            V((rows, share, columns), BF), V((rows, share, columns), BF),
            V((mine, columns, columns), BF),
            dma((6,)), dma((3,)), dma((3,)), dma, dma, dma((4,)), dma((3 + width,)), dma((4,)),
            dma((rows,)), dma((rows,)), dma((rows,)), dma((rows,)), dma, dma, dma,
            pltpu.SemaphoreType.REGULAR, pltpu.SemaphoreType.REGULAR,
        ],
        compiler_params=pltpu.CompilerParams(
            collective_id=1, has_side_effects=True, vmem_limit_bytes=52 << 20
        ),
    )(traces_in, w_value, w_gate, first_blocks, second_blocks, cotangent)
    return pl.pallas_call(
        write_kernel,
        out_shape=out_shape,
        in_specs=[vmem] * 4,
        out_specs=[hbm] * 4,
        scratch_shapes=[dma((4,))],
        compiler_params=pltpu.CompilerParams(vmem_limit_bytes=8 << 20),
    )(*[pltpu.with_memory_space_constraint(o, pltpu.VMEM) for o in outs])


def solution(mesh):
    big, weight = P("dp", "seq", None, None), P("seq", "dp", None)
    return jax.shard_map(
        on_device,
        mesh=mesh,
        in_specs=(big, P(), P(), weight, weight, big),
        out_specs=(big, big, weight, weight),
        check_vma=False,
    )
```

```python
import jax
import jax.numpy as jnp
from jax import lax
from jax.experimental import pallas as pl
from jax.experimental.pallas import tpu as pltpu
from jax.sharding import PartitionSpec as P

MESH = pl.DeviceIdType.MESH
BF = jnp.bfloat16
F32 = jnp.float32
NT = (((1,), (1,)), ((), ()))
TN = (((0,), (0,)), ((), ()))
NN = (((1,), (0,)), ((), ()))


def dot(a, b, dims=NN):
    return lax.dot_general(a, b, dims, preferred_element_type=F32)


def kernel(
    x_hbm, wv_hbm, wg_hbm, first_hbm, second_hbm, cot_hbm,
    mixed, gin, gf, gs_out,
    wv, wg, val, act, slope, part, first, second, tmp,
    send_a, send_b, cols_a, cols_b, send_c, send_d, rows_c, rows_d,
    gf_tmp, gf_own, gf_near, gf_near_in, gf_far, gf_far_in, gs,
    in_sem, f_send, f_recv, s_send, s_recv, ex_send, ex_recv, ex_own,
    near_send, near_recv, far_send, far_recv, gs_send, gs_recv, gs_own, group, ready,
):
    x, cot = mixed, gin
    width, length = lax.axis_size("dp"), lax.axis_size("seq")
    n = width * length
    traces, rows, columns, channels = x.shape
    mine = columns // n
    share = columns // width
    d, s = lax.axis_index("dp"), lax.axis_index("seq")
    me = s * width + d
    near = d + 1 - 2 * lax.rem(d, 2)
    far = lax.rem(d + 2, width)
    cross = lax.rem(near + 2, width)

    loads = [
        pltpu.make_async_copy(a, b, in_sem.at[i])
        for i, (a, b) in enumerate(
            [
                (x_hbm, x), (cot_hbm, cot), (wg_hbm, wg), (wv_hbm, wv),
                (first_hbm, first.at[:, pl.ds(pl.multiple_of(share * d, share), share), :]),
                (
                    second_hbm.at[pl.ds(mine * d, mine)],
                    second.at[:, pl.ds(pl.multiple_of(share * d, share), share), :],
                ),
            ]
        )
    ]
    for load in loads:
        load.start()

    barrier = pltpu.get_barrier_semaphore()

    def signal(sem, to_dp, to_seq):
        pl.semaphore_signal(sem, inc=1, device_id=(to_dp, to_seq), device_id_type=MESH)

    @pl.when(d != 0)
    def _():
        signal(barrier, 0, s)

    @pl.when(d == 0)
    def _():
        pl.semaphore_wait(barrier, width - 1)
        for other in range(1, width):
            signal(group, other, s)

    @pl.when(d != 0)
    def _():
        pl.semaphore_wait(group, 1)

    def remote(a, b, send, recv, to_dp, to_seq):
        return pltpu.make_async_remote_copy(
            a, b, send, recv, device_id=(to_dp, to_seq), device_id_type=MESH
        )

    def block(owner):
        return pl.ds(pl.multiple_of(share * owner, share), share)

    first_far = remote(first_hbm, first.at[:, block(d), :], f_send.at[0], f_recv.at[0], far, s)
    first_near = remote(first_hbm, first.at[:, block(d), :], f_send.at[1], f_recv.at[1], near, s)
    first_pass = remote(
        first.at[:, block(far), :], first.at[:, block(far), :], f_send.at[2], f_recv.at[2], near, s
    )
    first_far.start()
    first_near.start()

    def second_to(other):
        return remote(
            second_hbm.at[pl.ds(mine * other, mine)], second.at[:, block(d), :],
            s_send, s_recv, other, s,
        )

    for other in (far, cross, near):
        second_to(other).start()

    @pl.when(d == 1)
    def _():
        def greet(k, carry):
            signal(barrier, 1, lax.rem(s + k, length))
            return carry

        lax.fori_loop(1, length, greet, 0)

    def pieces_wait(sem):
        rest = send_a.at[:, pl.ds(0, columns - mine)]
        pltpu.make_async_copy(rest, rest, sem).wait()

    def to_columns(buf, out, which):
        def target(o):
            return o.at[pl.ds(traces * d, traces), :, pl.ds(pl.multiple_of(rows * s, rows), rows), :]

        own = pltpu.make_async_copy(
            buf.at[:, pl.ds(mine * me, mine)], target(out), ex_own.at[which]
        )
        own.start()

        def send(k, carry):
            e = lax.rem(me + k, n)
            remote(
                buf.at[:, pl.ds(mine * e, mine)], target(out),
                ex_send.at[which], ex_recv.at[which], lax.rem(e, width), e // width,
            ).start()
            return carry

        lax.fori_loop(1, n, send, 0)
        return own

    def source(buf, e_dp, e_seq):
        return buf.at[
            pl.ds(traces * e_dp, traces), :, pl.ds(pl.multiple_of(rows * e_seq, rows), rows), :
        ]

    def to_rows(buf, out, which, e_dp, first_k):
        def send(k, carry):
            e_seq = lax.rem(s + k, length)
            remote(
                source(buf, e_dp, e_seq), out.at[:, pl.ds(mine * me, mine)],
                ex_send.at[which], ex_recv.at[which], e_dp, e_seq,
            ).start()
            return carry

        lax.fori_loop(first_k, length, send, 0)

    step = 64

    def pack(buf):
        def body(i, carry):
            t, k = i // (columns // step), lax.rem(i, columns // step)
            rows_here = pl.ds(pl.multiple_of(k * step * rows, step * rows), step * rows)
            y = tmp[t, rows_here, :].reshape(step, rows, channels)
            buf[t, pl.ds(k * step, step)] = y.astype(BF)
            return carry

        lax.fori_loop(0, traces * (columns // step), body, 0)

    def unpack(buf):
        def body(i, carry):
            t, k = i // (columns // step), lax.rem(i, columns // step)
            rows_here = pl.ds(pl.multiple_of(k * step * rows, step * rows), step * rows)
            y = buf[t, pl.ds(k * step, step)].astype(F32)
            tmp[t, rows_here, :] = y.reshape(step * rows, channels)
            return carry

        lax.fori_loop(0, traces * (columns // step), body, 0)

    def row(p):
        return pl.ds(p, columns, stride=rows)

    loads[0].wait()
    loads[1].wait()
    loads[2].wait()

    def gate(i, carry):
        t, p = i // rows, lax.rem(i, rows)
        g = dot(x[t, p], wg[...])
        sig = jax.nn.sigmoid(g)
        a = g * sig
        c = cot[t, p].astype(F32)
        act[t, p] = a
        slope[t, p] = c * sig * (1.0 + g * (1.0 - sig))
        tmp[t, row(p), :] = c * a
        return carry

    lax.fori_loop(0, rows, gate, 0)

    @pl.when(d == 1)
    def _():
        pl.semaphore_wait(barrier, length - 1)
        for other in (0, *range(2, width)):
            signal(ready, other, s)

    lax.fori_loop(rows, traces * rows, gate, 0)
    pack(send_a)

    @pl.when(d != 1)
    def _():
        pl.semaphore_wait(ready, 1)

    own_a = to_columns(send_a, cols_a, 0)
    loads[3].wait()

    def value(i, carry):
        t, p = i // rows, lax.rem(i, rows)
        val[t, p] = dot(x[t, p], wv[...]).astype(BF)
        return carry

    lax.fori_loop(0, traces * rows, value, 0)

    loads[4].wait()
    first_far.wait_recv()
    first_pass.start()
    first_near.wait_recv()
    first_pass.wait_recv()

    def both(ref, p):
        return jnp.concatenate([ref[t, p] for t in range(traces)], axis=1)

    def mix_rows(p, carry):
        o = dot(first[p], both(val, p))
        for t in range(traces):
            tmp[t, row(p), :] = o[:, t * channels : (t + 1) * channels]
        return carry

    lax.fori_loop(0, rows, mix_rows, 0)
    pack(send_b)
    own_b = to_columns(send_b, cols_b, 1)

    loads[5].wait()
    half = second.at[:, pl.ds(0, share * (width - 1)), :]
    pltpu.make_async_copy(half, half, s_recv).wait()

    def columns_back(cols, buf, out, which, dims):
        owns = []
        for k in range(width):
            e_dp = lax.rem(d + k, width)

            def mix(q, carry):
                r = jnp.concatenate(
                    [cols[traces * e_dp + t, q] for t in range(traces)], axis=1
                )
                o = dot(second[q], r, dims).astype(BF)
                for t in range(traces):
                    buf[traces * e_dp + t, q] = o[:, t * channels : (t + 1) * channels]
                return carry

            lax.fori_loop(0, mine, mix, 0)
            if k == 0:
                own = pltpu.make_async_copy(
                    source(buf, d, s), out.at[:, pl.ds(mine * me, mine)], ex_own.at[which]
                )
                own.start()
                owns.append(own)
            to_rows(buf, out, which, e_dp, 1 if k == 0 else 0)
        return owns[0]

    own_a.wait()
    pieces_wait(ex_recv.at[0])
    own_c = columns_back(cols_a, send_c, rows_c, 2, TN)
    own_b.wait()
    pieces_wait(ex_recv.at[1])
    own_d = columns_back(cols_b, send_d, rows_d, 3, NN)

    scale = 1.0 / (traces * width)

    def second_grad(q, carry):
        a = jnp.concatenate([cols_a[t, q] for t in range(traces * width)], axis=1)
        b = jnp.concatenate([cols_b[t, q] for t in range(traces * width)], axis=1)
        gs[q] = (dot(a, b, NT) * scale).astype(BF)
        return carry

    lax.fori_loop(0, mine, second_grad, 0)

    def gs_to(other):
        return remote(
            gs.at[:, block(other), :], gs_out.at[pl.ds(mine * d, mine)], gs_send, gs_recv, other, s
        )

    gs_mine = pltpu.make_async_copy(gs.at[:, block(d), :], gs_out.at[pl.ds(mine * d, mine)], gs_own)
    gs_mine.start()

    own_c.wait()
    pieces_wait(ex_recv.at[2])
    unpack(rows_c)

    def near_copy(p):
        return remote(gf_near.at[p], gf_near_in.at[p], near_send.at[p], near_recv.at[p], near, s)

    def far_copy(p):
        return remote(gf_far.at[p], gf_far_in.at[p], far_send.at[p], far_recv.at[p], far, s)

    def rows_back(p, carry):
        r = jnp.concatenate([tmp[t, row(p), :] for t in range(traces)], axis=1).astype(BF)
        gf_tmp[...] = dot(r, both(val, p), NT)
        gf_own[p, 0] = gf_tmp[block(d), :]
        gf_own[p, 1] = gf_tmp[block(far), :]
        gf_near[p, 0] = gf_tmp[block(near), :].astype(BF)
        gf_near[p, 1] = gf_tmp[block(cross), :].astype(BF)
        near_copy(p).start()
        v = dot(first[p], r, TN).astype(BF)
        for t in range(traces):
            part[t, p] = dot(v[:, t * channels : (t + 1) * channels], wv[...], NT)
        return carry

    lax.fori_loop(0, rows, rows_back, 0)

    def reduce_near(p, carry):
        near_copy(p).wait_recv()
        gf_far[p] = (gf_own[p, 1] + gf_near_in[p, 1].astype(F32)).astype(BF)
        gf_own[p, 0] = gf_own[p, 0] + gf_near_in[p, 0].astype(F32)
        return carry

    lax.fori_loop(0, rows, reduce_near, 0)

    def send_far(p, carry):
        far_copy(p).start()
        return carry

    lax.fori_loop(0, rows, send_far, 0)

    own_d.wait()
    pieces_wait(ex_recv.at[3])
    for other in (far, cross, near):
        gs_to(other).start()
    unpack(rows_d)

    def finish(i, carry):
        t, p = i // rows, lax.rem(i, rows)
        c = tmp[t, row(p), :]
        mixed[t, p] = (c * act[t, p]).astype(BF)
        g = (c * slope[t, p]).astype(BF)
        gin[t, p] = (part[t, p] + dot(g, wg[...], NT)).astype(BF)
        return carry

    lax.fori_loop(0, traces * rows, finish, 0)

    def reduce_far(p, carry):
        far_copy(p).wait_recv()
        gf[p] = ((gf_own[p, 0] + gf_far_in[p].astype(F32)) * scale).astype(BF)
        return carry

    lax.fori_loop(0, rows, reduce_far, 0)

    first_far.wait_send()
    first_near.wait_send()
    first_pass.wait_send()
    pltpu.make_async_copy(half, half, s_send).wait()
    for which in range(4):
        pieces_wait(ex_send.at[which])

    def sent(p, carry):
        far_copy(p).wait_send()
        near_copy(p).wait_send()
        return carry

    lax.fori_loop(0, rows, sent, 0)
    gs_mine.wait()
    three = gs.at[:, pl.ds(0, share * (width - 1)), :]
    pltpu.make_async_copy(three, three, gs_send).wait()
    pltpu.make_async_copy(three, three, gs_recv).wait()


def write_kernel(*refs):
    sem = refs[-1]
    half = len(refs) // 2
    copies = [
        pltpu.make_async_copy(a, b, sem.at[i]) for i, (a, b) in enumerate(zip(refs[:half], refs[half:-1]))
    ]
    for copy in copies:
        copy.start()
    for copy in copies:
        copy.wait()


def on_device(traces_in, w_value, w_gate, first_blocks, second_blocks, cotangent):
    width, length = lax.axis_size("dp"), lax.axis_size("seq")
    traces, rows, columns, channels = traces_in.shape
    mine, share = columns // (width * length), columns // width
    by_row = (traces, columns, rows, channels)
    by_column = (traces * width, mine, rows * length, channels)
    hbm = pl.BlockSpec(memory_space=pl.ANY)
    dma = pltpu.SemaphoreType.DMA
    V = pltpu.VMEM
    shape = traces_in.shape
    vmem = pl.BlockSpec(memory_space=pltpu.VMEM)
    out_shape = [
        jax.ShapeDtypeStruct(shape, BF),
        jax.ShapeDtypeStruct(shape, BF),
        jax.ShapeDtypeStruct(first_blocks.shape, BF),
        jax.ShapeDtypeStruct(second_blocks.shape, BF),
    ]
    outs = pl.pallas_call(
        kernel,
        out_shape=[pltpu.VMEM(o.shape, o.dtype) for o in out_shape],
        in_specs=[hbm] * 6,
        out_specs=[vmem] * 4,
        scratch_shapes=[
            V(w_value.shape, BF), V(w_gate.shape, BF), V(shape, BF),
            V(shape, F32), V(shape, F32), V(shape, F32),
            V((rows, columns, columns), BF), V((mine, columns, columns), BF),
            V((traces, columns * rows, channels), F32),
            V(by_row, BF), V(by_row, BF), V(by_column, BF), V(by_column, BF),
            V(by_column, BF), V(by_column, BF), V(by_row, BF), V(by_row, BF),
            V((columns, columns), F32), V((rows, 2, share, columns), F32),
            V((rows, 2, share, columns), BF), V((rows, 2, share, columns), BF),
            V((rows, share, columns), BF), V((rows, share, columns), BF),
            V((mine, columns, columns), BF),
            dma((6,)), dma((3,)), dma((3,)), dma, dma, dma((4,)), dma((4,)), dma((4,)),
            dma((rows,)), dma((rows,)), dma((rows,)), dma((rows,)), dma, dma, dma,
            pltpu.SemaphoreType.REGULAR, pltpu.SemaphoreType.REGULAR,
        ],
        compiler_params=pltpu.CompilerParams(
            collective_id=1, has_side_effects=True, vmem_limit_bytes=52 << 20
        ),
    )(traces_in, w_value, w_gate, first_blocks, second_blocks, cotangent)
    return pl.pallas_call(
        write_kernel,
        out_shape=out_shape,
        in_specs=[vmem] * 4,
        out_specs=[hbm] * 4,
        scratch_shapes=[dma((4,))],
        compiler_params=pltpu.CompilerParams(vmem_limit_bytes=8 << 20),
    )(*[pltpu.with_memory_space_constraint(o, pltpu.VMEM) for o in outs])


def solution(mesh):
    big, weight = P("dp", "seq", None, None), P("seq", "dp", None)
    return jax.shard_map(
        on_device,
        mesh=mesh,
        in_specs=(big, P(), P(), weight, weight, big),
        out_specs=(big, big, weight, weight),
        check_vma=False,
    )
```
